32 devices in a mesh: fsdp: 16 (over z, x, core), tensor: 2 (over y).
Axes of the slice: x: 2, y: 2, z: 4, core: 2. Of those that a mesh axis runs over, the one named last changes fastest.
Arguments:
- hidden: bfloat16 [2, 1024, 11264], P(None, 'fsdp', 'tensor'), may hold values from -6 to 6
- down_weight: bfloat16 [11264, 8192], P('tensor', 'fsdp'), may hold values from -0.0546875 to 0.0546875
- probes: bfloat16 [2, 11264, 8192], P(None, 'tensor', 'fsdp'), may hold values from -6 to 6
- teacher: float32 [2, 1024, 8192], P(None, 'tensor', 'fsdp'), may hold values from -6 to 6
- token_ids: int32 [2, 1024], replicated, may hold values from 0 to 31999, as said below
Outputs:
- sketch: float32 [2, 11264, 8192], P(None, 'tensor', 'fsdp')
- diagonal: float32 [11264, 8192], P('tensor', 'fsdp')
The draws below stay inside these ranges and needn't reach their ends.
Inputs may be any that keep to these rules, and one draw needn't show every extreme that they name: `token_ids`: id 0 marks a padding token, which carries no loss; other tokens hold ids of 1 to 31999.
All inputs are finite; a program needn't handle non-finite values.
Results may differ from the reference program's by a relative error of at most 0.015.
Values may be sent and summed in bfloat16 or wider, within the bound.
No kernel may reach another device: no remote copies, remote signals or barrier semaphores. Data moves between devices by JAX's collectives and lax.ppermute only.
A program may use at most 192 MiB of HBM per device.

```python
import jax
import jax.numpy as jnp
from jax import lax

D = 8192
VOCAB = 32000
HID = 11264
PROBES = 2
BATCHES = 2
ROWS = 1024
N_TENSOR = 2


def draw_token_ids(key, part):
    words_key, keep_key = jax.random.split(jax.random.fold_in(key, 7))
    vocab_words = jax.random.randint(words_key, (BATCHES, ROWS), 1, VOCAB)
    padded = jax.random.randint(keep_key, (BATCHES, ROWS), 0, 4)
    return jnp.where(padded == 0, 0, vocab_words).astype(jnp.int32)


def level_of(rng, shape, shards, low, top_value):
    factor_of = 1.0
    for position, parts in shards:
        steps = jax.random.uniform(jax.random.fold_in(jax.random.fold_in(rng, 6), position), (parts,), jnp.float32, low / len(shards), top_value / len(shards))
        factor_of = factor_of * jnp.repeat(jnp.exp(steps), shape[position] // parts).reshape((-1,) + (1,) * (len(shape) - 1 - position))
    return factor_of


def noise(stream_key, extent, spread, reach, cuts=(), dtype=jnp.bfloat16):
    entries = spread * jax.random.normal(stream_key, extent, jnp.float32)
    if cuts:
        entries = entries * level_of(stream_key, extent, cuts, -0.22, 0.18)
    return jnp.clip(entries, -reach, reach).astype(dtype)


def setup_inputs(seed: int = 0) -> dict:
    key_of = jax.random.split(jax.random.key(seed), 6)
    hidden = noise(key_of[0], (BATCHES, ROWS, HID), 1.0, 6.0, ((1, 16), (2, 2)))
    down_weight = noise(key_of[1], (HID, D), HID ** -0.5, 0.0546875, ((0, 2), (1, 16)))
    probes = noise(key_of[2], (PROBES, HID, D), 1.0, 6.0, ((1, 2), (2, 16)))
    teacher = noise(key_of[3], (BATCHES, ROWS, D), 1.0, 6.0, ((1, 2), (2, 16)), jnp.float32)
    token_ids = draw_token_ids(jax.random.fold_in(key_of[5], 71), 0)
    return dict(hidden=hidden, down_weight=down_weight, probes=probes, teacher=teacher, token_ids=token_ids)


def weighted(totals, teacher, labels, columns, probe_count, normalizer):
    outputs = totals[:, :columns]
    tangents = totals[:, columns:].reshape(totals.shape[0], probe_count, columns)
    residue = outputs - teacher
    curvature = jnp.where(labels[:, None] != 0, 1.0, 0.0).astype(jnp.float32) * jnp.power(1.0 + residue * residue, -1.5) / normalizer
    scaled = tangents * curvature[:, None, :]
    return scaled.reshape(totals.shape[0], probe_count * columns).astype(jnp.bfloat16)


def reference(hidden, down_weight, probes, teacher, token_ids):
    part_width = HID // N_TENSOR
    stacked = jnp.concatenate([down_weight] + [probes[probe_index] for probe_index in range(PROBES)], axis=1)
    normalizer = float(BATCHES * ROWS)
    sketch = jnp.zeros((HID, PROBES * D), jnp.float32)
    for batch_index in range(BATCHES):
        hidden_rows = hidden[batch_index]
        totals = jnp.zeros((ROWS, (PROBES + 1) * D), jnp.float32)
        for block_index in range(N_TENSOR):
            low = block_index * part_width
            partial_term = jnp.dot(hidden_rows[:, low:low + part_width], stacked[low:low + part_width], preferred_element_type=jnp.float32)
            totals = totals + lax.optimization_barrier(partial_term.astype(jnp.bfloat16)).astype(jnp.float32)
        factors = weighted(totals, teacher[batch_index], token_ids[batch_index], D, PROBES, normalizer)
        sketch = sketch + jnp.dot(hidden_rows.T, factors, preferred_element_type=jnp.float32)
    result = sketch.reshape(HID, PROBES, D).transpose(1, 0, 2)
    diagonal = jnp.mean(probes.astype(jnp.float32) * result, axis=0)
    return result, diagonal
```

```python
import functools

import jax
import jax.numpy as jnp
from jax import lax
from jax.experimental import pallas as pl
from jax.experimental.pallas import tpu as pltpu
from jax.sharding import PartitionSpec as P


SIDE, SELF, BASE, TABLE = 0, 2, 3, 4
F32, BF16 = jnp.float32, jnp.bfloat16
ROWS = (((0,), (0,)), ((), ()))


def weighted(totals, teacher, labels, columns, probe_count, normalizer):
    outputs = totals[:, :columns]
    tangents = totals[:, columns:].reshape(totals.shape[0], probe_count, columns)
    residue = outputs - teacher
    curvature = (
        jnp.where(labels[:, None] != 0, 1.0, 0.0).astype(jnp.float32)
        * jnp.power(1.0 + residue * residue, -1.5)
        / normalizer
    )
    scaled = tangents * curvature[:, None, :]
    return scaled.reshape(totals.shape[0], probe_count * columns).astype(jnp.bfloat16)


def general(hidden, down_weight, probes, teacher, token_ids):
    probe_count = probes.shape[0]
    columns = down_weight.shape[1]
    batches = hidden.shape[0]
    rows_all = hidden.shape[1] * lax.axis_size("fsdp")
    share_rows = rows_all // lax.axis_size("tensor")
    normalizer = float(batches * rows_all)
    stacked = jnp.concatenate(
        [down_weight] + [probes[probe_index] for probe_index in range(probe_count)], axis=1
    )
    start_row = lax.axis_index("tensor") * share_rows
    gathered_all = lax.all_gather(hidden, "fsdp", axis=1, tiled=True)

    def step(sketch, batch):
        gathered, targets, ids = batch
        partial_value = jnp.dot(gathered, stacked, preferred_element_type=jnp.float32)
        shares = lax.psum_scatter(
            partial_value.astype(jnp.bfloat16), "tensor", scatter_dimension=0, tiled=True
        ).astype(jnp.float32)
        labels = lax.dynamic_slice_in_dim(ids, start_row, share_rows, 0)
        scaled = weighted(shares, targets, labels, columns, probe_count, normalizer)
        factors = lax.all_gather(scaled, "tensor", axis=0, tiled=True)
        update = [
            lax.dot_general(
                gathered,
                factors[:, k * columns : (k + 1) * columns],
                ROWS,
                preferred_element_type=jnp.float32,
            )
            for k in range(probe_count)
        ]
        return sketch + jnp.stack(update), None

    sketch = jnp.zeros((probe_count,) + down_weight.shape, jnp.float32)
    sketch, _ = lax.scan(step, sketch, (gathered_all, teacher, token_ids))
    diagonal = jnp.mean(probes.astype(jnp.float32) * sketch, axis=0)
    return (sketch, diagonal)


def call(kernel, meta, grid, in_specs, out_specs, out_shape, scratch, cost, name, *operands):
    limit = 32 if name == "finish" else 12
    flops, moved = cost
    return pl.pallas_call(
        kernel,
        grid_spec=pltpu.PrefetchScalarGridSpec(
            num_scalar_prefetch=1,
            grid=(grid,),
            in_specs=in_specs,
            out_specs=out_specs,
            scratch_shapes=scratch,
        ),
        out_shape=out_shape,
        cost_estimate=pl.CostEstimate(flops=flops, bytes_accessed=moved, transcendentals=0),
        compiler_params=pltpu.CompilerParams(vmem_limit_bytes=limit << 20),
    )(meta, *operands)


def picker(ids, keep):
    tokens = ids.shape[1]
    active = (ids != 0).astype(F32)
    upper = lax.broadcasted_iota(jnp.int32, (tokens, tokens), 0)
    upper = (upper <= lax.broadcasted_iota(jnp.int32, (tokens, tokens), 1)).astype(BF16)
    wide = jnp.broadcast_to(active, (8, tokens)).astype(BF16)
    rank = jnp.dot(wide, upper, preferred_element_type=F32)[:1] - 1.0
    slots = lax.broadcasted_iota(jnp.int32, (keep, tokens), 0).astype(F32)
    hit = (slots == jnp.broadcast_to(rank, (keep, tokens))).astype(F32)
    return (hit * jnp.broadcast_to(active, (keep, tokens))).astype(BF16)


def pack_kernel(meta, ids_ref, hidden_ref, main_ref, spare_ref):
    main, spare = main_ref.shape[0], spare_ref.shape[0]
    pick = picker(ids_ref[0], main + spare)
    rows = jnp.concatenate([hidden_ref[b] for b in range(hidden_ref.shape[0])], axis=0)
    kept = jnp.dot(pick, rows, preferred_element_type=F32).astype(BF16)
    main_ref[...] = kept[:main]
    spare_ref[...] = kept[main:]


def pack(meta, ids, hidden, main, spare, tile):
    batches, rows, units = hidden.shape
    return call(
        pack_kernel,
        meta,
        units // tile,
        [
            pl.BlockSpec((1, 1, batches * rows), lambda i, s: (s[SELF], 0, 0)),
            pl.BlockSpec((batches, rows, tile), lambda i, s: (0, 0, i)),
        ],
        [
            pl.BlockSpec((main, tile), lambda i, s: (0, i)),
            pl.BlockSpec((spare, tile), lambda i, s: (0, i)),
        ],
        [
            jax.ShapeDtypeStruct((main, units), BF16),
            jax.ShapeDtypeStruct((spare, units), BF16),
        ],
        [],
        (2 * (main + spare) * batches * rows * units, 4 * batches * rows * units),
        "pack",
        ids,
        hidden,
    )


def aim_kernel(meta, ids_ref, teacher_ref, kept_ref, sent_ref):
    keep, half = kept_ref.shape[1:]
    pick = picker(ids_ref[0], keep)
    rows = jnp.concatenate([teacher_ref[b] for b in range(teacher_ref.shape[0])], axis=0)
    picked = jnp.dot(pick, rows.astype(BF16), preferred_element_type=F32)
    low, high = picked[:, :half], picked[:, half:]
    first = meta[SIDE] == 0
    kept_ref[0] = jnp.where(first, low, high).astype(BF16)
    sent_ref[0] = jnp.where(first, high, low).astype(BF16)


def aim(meta, ids, teacher, owners, keep):
    batches, rows, columns = teacher.shape
    each, half = rows // owners, columns // 2
    out = jax.ShapeDtypeStruct((owners, keep, half), BF16)
    return call(
        aim_kernel,
        meta,
        owners,
        [
            pl.BlockSpec((1, 1, batches * each), lambda i, s: (s[BASE] + i, 0, 0)),
            pl.BlockSpec((batches, each, columns), lambda i, s: (0, i, 0)),
        ],
        [pl.BlockSpec((1, keep, half), lambda i, s: (i, 0, 0))] * 2,
        [out, out],
        [],
        (2 * owners * keep * batches * each * columns, 8 * batches * rows * columns),
        "aim",
        ids,
        teacher,
    )


def spare_kernel(main, meta, ids_ref, rows_ref, kept_ref, got_ref, out_ref, wanted_ref):
    room = out_ref.shape[0]
    owners, keep, half = kept_ref.shape
    count = rows_ref.shape[0]
    spare = keep - main
    active = (ids_ref[:, 0] != 0).astype(BF16)
    fsdp = active.shape[0]
    lane = lax.broadcasted_iota(jnp.int32, (fsdp, count), 1)
    whose = lax.broadcasted_iota(jnp.int32, (fsdp, count), 0)
    spread = ((lane >= whose * spare) & (lane < (whose + 1) * spare)).astype(BF16)
    counts = lax.dot_general(active, spread, ROWS, preferred_element_type=F32)
    counts = jnp.sum(counts, axis=0, keepdims=True)
    order = lax.broadcasted_iota(jnp.int32, (1, count), 1) % spare
    used = (counts > (order + main).astype(F32)).astype(jnp.int32)
    pick = picker(used, room)
    out_ref[...] = jnp.dot(pick, rows_ref[...], preferred_element_type=F32).astype(BF16)

    @pl.when(pl.program_id(0) == 0)
    def _():
        kept = kept_ref[:, main:].reshape(owners * spare, half)
        got = got_ref[:, main:].reshape(owners * spare, half)
        first = meta[SIDE] == 0
        rows = jnp.concatenate(
            [jnp.where(first, kept, got), jnp.where(first, got, kept)], axis=0
        )
        wanted_ref[...] = jnp.dot(pick, rows, preferred_element_type=F32).astype(BF16)


def spare_rows(meta, ids, rows, kept, got, main, room, tile):
    count, units = rows.shape
    half = kept.shape[2]
    whole = lambda a: pl.BlockSpec(a.shape, lambda i, s: (0,) * a.ndim)
    return call(
        functools.partial(spare_kernel, main),
        meta,
        units // tile,
        [whole(ids), pl.BlockSpec((count, tile), lambda i, s: (0, i)), whole(kept), whole(got)],
        [
            pl.BlockSpec((room, tile), lambda i, s: (0, i)),
            pl.BlockSpec((room, half), lambda i, s: (0, 0)),
        ],
        [
            jax.ShapeDtypeStruct((room, units), BF16),
            jax.ShapeDtypeStruct((room, half), BF16),
        ],
        [],
        (2 * count * room * units, 2 * (count + room) * units),
        "spare",
        ids,
        rows,
        kept,
        got,
    )


def halves_kernel(meta, weight_ref, probes_ref, theirs_ref, ours_ref):
    half = weight_ref.shape[1] // 2
    first = meta[SIDE] == 0
    for j in range(1 + probes_ref.shape[0]):
        weight = weight_ref[...] if j == 0 else probes_ref[j - 1]
        at = slice(j * half, (j + 1) * half)
        theirs_ref[:, at] = jnp.where(first, weight[:, half:], weight[:, :half])
        ours_ref[:, at] = jnp.where(first, weight[:, :half], weight[:, half:])


def halves(meta, down_weight, probes, tile):
    probe_count, units, columns = probes.shape
    width = (1 + probe_count) * columns // 2
    return call(
        halves_kernel,
        meta,
        units // tile,
        [
            pl.BlockSpec((tile, columns), lambda i, s: (i, 0)),
            pl.BlockSpec((probe_count, tile, columns), lambda i, s: (0, i, 0)),
        ],
        [pl.BlockSpec((tile, width), lambda i, s: (i, 0))] * 2,
        [jax.ShapeDtypeStruct((units, width), BF16)] * 2,
        [],
        (0, 8 * units * width),
        "halves",
        down_weight,
        probes,
    )


def factor_kernel(place, normalizer, meta, ours_ref, got_ref, kept_ref, crossed_ref, out_ref):
    half = kept_ref.shape[2]
    step = pl.program_id(0)
    wanted = jnp.where(meta[place + 3 * step + 2] == 0, kept_ref[0], crossed_ref[0])
    totals = ours_ref[...].astype(F32) + got_ref[...].astype(F32)
    residue = totals[:, :half] - wanted.astype(F32)
    root = lax.rsqrt(1.0 + residue * residue)
    curvature = root * root * root * (1.0 / normalizer)
    for j in range(out_ref.shape[1] // half):
        tangent = totals[:, (j + 1) * half : (j + 2) * half]
        out_ref[:, j * half : (j + 1) * half] = (curvature * tangent).astype(BF16)


def factor(meta, place, ours, got, kept, crossed, main, normalizer):
    rows, width = ours.shape
    half = kept.shape[2]
    return call(
        functools.partial(factor_kernel, place, normalizer),
        meta,
        rows // main,
        [
            pl.BlockSpec((main, width), lambda i, s: (i, 0)),
            pl.BlockSpec((main, width), lambda i, s: (i, 0)),
            pl.BlockSpec((1, main, half), lambda i, s: (s[place + 3 * i], 0, 0)),
            pl.BlockSpec((1, main, half), lambda i, s: (s[place + 3 * i + 1], 0, 0)),
        ],
        pl.BlockSpec((main, width - half), lambda i, s: (i, 0)),
        jax.ShapeDtypeStruct((rows, width - half), BF16),
        [],
        (20 * rows * width, 8 * rows * width),
        "factor",
        ours,
        got,
        kept,
        crossed,
    )


def placed(meta, ours_refs, other_refs, placed_ref, probe_count):
    first = meta[SIDE] == 0
    half = ours_refs[0].shape[1] // probe_count
    start = 0
    for ours_ref, other_ref in zip(ours_refs, other_refs):
        rows = ours_ref.shape[0]
        for k in range(probe_count):
            a = ours_ref[:, k * half : (k + 1) * half]
            b = other_ref[:, k * half : (k + 1) * half]
            low = slice(2 * k * half, (2 * k + 1) * half)
            high = slice((2 * k + 1) * half, (2 * k + 2) * half)
            placed_ref[start : start + rows, low] = jnp.where(first, a, b)
            placed_ref[start : start + rows, high] = jnp.where(first, b, a)
        start += rows


def backward_kernel(groups, meta, *refs):
    block_refs, refs = refs[:groups], refs[groups:]
    ours_refs, refs = refs[:groups], refs[groups:]
    other_refs, refs = refs[:groups], refs[groups:]
    probes_ref, sketch_ref, diagonal_ref, placed_ref = refs
    probe_count, _, columns = sketch_ref.shape

    @pl.when(pl.program_id(0) == 0)
    def _():
        placed(meta, ours_refs, other_refs, placed_ref, probe_count)

    rows = jnp.concatenate([ref[...] for ref in block_refs], axis=0)
    diagonal = jnp.zeros(diagonal_ref.shape, F32)
    for k in range(probe_count):
        factors = placed_ref[:, k * columns : (k + 1) * columns]
        sketch = lax.dot_general(rows, factors, ROWS, preferred_element_type=F32)
        sketch_ref[k] = sketch
        diagonal = diagonal + probes_ref[k].astype(F32) * sketch
    diagonal_ref[...] = diagonal * (1.0 / probe_count)


def backward(meta, blocks, ours, others, probes, tile):
    probe_count, units, columns = probes.shape
    rows = sum(b.shape[0] for b in blocks)
    whole = lambda a: pl.BlockSpec(a.shape, lambda i, s: (0, 0))
    wide = pl.BlockSpec((probe_count, tile, columns), lambda i, s: (0, i, 0))
    return call(
        functools.partial(backward_kernel, len(blocks)),
        meta,
        units // tile,
        [pl.BlockSpec((b.shape[0], tile), lambda i, s: (0, i)) for b in blocks]
        + [whole(a) for a in ours + others]
        + [wide],
        [wide, pl.BlockSpec((tile, columns), lambda i, s: (i, 0))],
        [
            jax.ShapeDtypeStruct((probe_count, units, columns), F32),
            jax.ShapeDtypeStruct((units, columns), F32),
        ],
        [pltpu.VMEM((rows, probe_count * columns), BF16)],
        (
            2 * rows * units * probe_count * columns,
            units * (2 * rows + columns * (6 * probe_count + 4)),
        ),
        "finish",
        *blocks,
        *ours,
        *others,
        probes,
    )


def layout(fsdp):
    planes = fsdp // 4

    def at(plane, side, core):
        return (plane * 2 + side) * 2 + core

    spots = [(p, s, c) for p in range(planes) for s in range(2) for c in range(2)]
    ring = list(range(0, planes, 2)) + list(range(1, planes, 2))[::-1]
    place = {p: i for i, p in enumerate(ring)}
    onward = [(at(p, s, c), at(ring[(place[p] + 1) % planes], s, c)) for p, s, c in spots]
    aside = [(at(p, s, c), at(p, 1 - s, c)) for p, s, c in spots]
    sibling = [(at(p, s, c), at(p, s, 1 - c)) for p, s, c in spots]

    def origin(hops, cross):
        same, other = [], []
        for p, s, c in spots:
            plane = ring[(place[p] - hops) % planes]
            side = 1 - s if cross else s
            same.append(at(plane, side, c))
            other.append(at(plane, side, 1 - c))
        return [same, other]

    return planes, onward, aside, sibling, origin


def packed(hidden, down_weight, probes, teacher, ids, main, spare):
    _, units, _ = probes.shape
    batches, rows_own = hidden.shape[:2]
    fsdp = lax.axis_size("fsdp")
    me, side = lax.axis_index("fsdp"), lax.axis_index("tensor")
    normalizer = float(batches * rows_own * fsdp)
    owners = fsdp // 2
    planes, onward, aside, sibling, origin = layout(fsdp)
    swap = [(0, 1), (1, 0)]
    tile = units // 4 if units % 512 == 0 else 512

    steps = [(0, False)]
    for hop in range(1, planes):
        steps += [(hop - 1, True), (hop, False)]
    steps.append((planes - 1, True))
    origins = [source for hops, cross in steps for source in origin(hops, cross)]
    table = jnp.array(origins, jnp.int32).T[me]
    local = table % owners
    crossed = (table // owners != side).astype(jnp.int32)
    at = 4 * planes - 6
    table = jnp.stack([local, local, crossed], axis=1)
    table = jnp.concatenate([table[:at], jnp.zeros((1, 3), jnp.int32), table[at:]], axis=0)
    meta = jnp.concatenate(
        [jnp.stack([side, 1 - side, me, side * owners]).astype(jnp.int32), table.reshape(-1)]
    )

    block, spared = pack(meta, ids, hidden, main, spare, tile)
    ring_blocks, cross_blocks = [block], []
    for hop in range(planes):
        cross_blocks.append(lax.ppermute(ring_blocks[hop], "fsdp", aside))
        if hop + 1 < planes:
            ring_blocks.append(lax.ppermute(ring_blocks[hop], "fsdp", onward))
    spared = lax.all_gather(spared, "fsdp", axis=0, tiled=True)

    kept, sent = aim(meta, ids, teacher, owners, main + spare)
    got = lax.ppermute(sent, "tensor", swap)
    extra, extra_wanted = spare_rows(meta, ids, spared, kept, got, main, main, tile)

    weights = halves(meta, down_weight, probes, 512)

    def pair(value):
        return [value, lax.ppermute(value, "fsdp", sibling)]

    groups = [("0", pair(ring_blocks[0]))]
    for hop in range(1, planes):
        blocks = pair(cross_blocks[hop - 1]) + pair(ring_blocks[hop])
        groups.append((str(hop), blocks))
    groups.insert(-1, ("s", [extra]))
    groups.append((str(planes), pair(cross_blocks[planes - 1])))

    joined, ours_all, other_all, place = [], [], [], TABLE
    for name, blocks in groups:
        rows = blocks[0] if len(blocks) == 1 else jnp.concatenate(blocks, axis=0)
        joined.append(rows)
        theirs = jnp.dot(rows, weights[0], preferred_element_type=F32).astype(BF16)
        arrived = lax.ppermute(theirs, "tensor", swap)
        ours = jnp.dot(rows, weights[1], preferred_element_type=F32).astype(BF16)
        aims = (extra_wanted[None],) * 2 if name == "s" else (kept, got)
        scaled = factor(meta, place, ours, arrived, *aims, main, normalizer)
        place += 3 * len(blocks)
        ours_all.append(scaled)
        other_all.append(lax.ppermute(scaled, "tensor", swap))
    return backward(meta, joined, ours_all, other_all, probes, 512)


def on_device(hidden, down_weight, probes, teacher, token_ids):
    fsdp, tensor = lax.axis_size("fsdp"), lax.axis_size("tensor")
    batches, rows_own, units = hidden.shape
    tokens = batches * rows_own
    columns = down_weight.shape[1]
    main, spare = tokens * 3 // 4, tokens // 8
    fits = tensor == 2 and fsdp % 4 == 0 and columns % 512 == 0 and units % 512 == 0
    fits = fits and tokens % 128 == 0 and rows_own % 16 == 0
    if not fits:
        return general(hidden, down_weight, probes, teacher, token_ids)
    ids = token_ids.reshape(batches, fsdp, rows_own).transpose(1, 0, 2).reshape(fsdp, 1, tokens)
    result = packed(hidden, down_weight, probes, teacher, ids, main, spare)
    counts = (ids != 0).astype(jnp.int32).sum(axis=(1, 2))
    over = jnp.maximum(counts - main, 0)
    heavy = jnp.any(over > spare) | (over.sum() > main)

    def again(carry):
        given = lax.optimization_barrier(
            (carry[0], hidden, down_weight, probes, teacher, token_ids)
        )
        return (jnp.array(False),) + general(*given[1:])

    _, sketch, diagonal = lax.while_loop(
        lambda carry: carry[0], again, (heavy,) + tuple(result)
    )
    return (sketch, diagonal)


def solution(mesh):
    in_specs = (
        P(None, "fsdp", "tensor"),
        P("tensor", "fsdp"),
        P(None, "tensor", "fsdp"),
        P(None, "tensor", "fsdp"),
        P(),
    )
    out_specs = (P(None, "tensor", "fsdp"), P("tensor", "fsdp"))
    return jax.shard_map(
        on_device, mesh=mesh, in_specs=in_specs, out_specs=out_specs, check_vma=False
    )
```
